256 devices in a mesh: grp: 8 (over y, core), dev: 32 (over z, x).
Axes of the slice: x: 4, y: 4, z: 8, core: 2. Of those that a mesh axis runs over, the one named last changes fastest.
Arguments:
- a_blocks: bfloat16 [8192, 7, 128, 128], P(('grp', 'dev')), may hold values from -0.5 to 0.5
- p_blocks: bfloat16 [8192, 128, 128], P(('grp', 'dev')), may hold values from -0.5 to 0.5
- neighbours: int32 [8192, 6], P(('grp', 'dev')), may hold values from 0 to 31
- coarse_slot: int32 [8192, 7], P(('grp', 'dev')), may hold values from 0 to 6
- owner: int32 [8192, 1], P(('grp', 'dev')), may hold values from 0 to 31; in each aligned block of 32 rows (0 to 31, 32 to 63, ...) at most 2 rows name the same one
- agg_local: int32 [8192], P(('grp', 'dev')), may hold values from 0 to 7
Outputs:
- coarse: bfloat16 [2048, 7, 128, 128], P(('grp', 'dev'))
The draws below stay inside these ranges and needn't reach their ends.
Inputs may be any that keep to these rules, and one draw needn't show every extreme that they name: Among the elements of one device at most 2 have the same owner, and in every draw some device has exactly 2 elements with one owner.
All inputs are finite; a program needn't handle non-finite values.
Results may differ from the reference program's by a relative error of at most 0.008.
Values may be sent and summed in bfloat16 or wider, within the bound.
A program may use at most 128 MiB of HBM per device.

```python
import math
import jax
import jax.numpy as jnp
import numpy as np
from jax import lax

BLK = 128
KC = 7
E_DEV = 32
AGG_DEV = 8
CAP = 2
OWNERS = 32
ELEMENTS = 8192
AGGS = 2048
N_GRP = 8
N_DEV = 32


def touch_ends(result, rng, least, high):
    extent = result.shape
    spot = [jax.random.randint(jax.random.fold_in(rng, axis), (), 0, extent[axis]) for axis in range(len(extent))]
    result = result.at[tuple(spot)].set(least)
    longest = extent.index(max(extent))
    spot[longest] = (spot[longest] + 1) % extent[longest]
    return result.at[tuple(spot)].set(high)


def levels(key, dims, split, smallest, high):
    gain = 1.0
    for axis_at, blocks in split:
        heights = jax.random.uniform(jax.random.fold_in(jax.random.fold_in(key, 6), axis_at), (blocks,), jnp.float32, smallest / len(split), high / len(split))
        gain = gain * jnp.repeat(jnp.exp(heights), dims[axis_at] // blocks).reshape((-1,) + (1,) * (len(dims) - 1 - axis_at))
    return gain


def assign_block(stream_key, own, number, rows, number_of, top, reach, slope):
    ranking = jax.random.permutation(stream_key, number_of)
    packed, usual = portions_of(number_of, rows * top, reach, slope, True), portions_of(number_of, rows * top, reach, slope, False)
    places = jnp.arange(number_of)

    def named(tallies, offset_by):
        used = int((tallies > 0).sum())
        fixed = max(1, used // 4)
        passed = fixed + (places - fixed + offset_by * (used - fixed)) % max(1, number_of - fixed)
        return jnp.zeros((number_of,), jnp.int32).at[ranking[jnp.where(places < fixed, places, passed)]].set(jnp.asarray(tallies, jnp.int32))

    tallies = jnp.where(number % 4 == 0, named(packed, number // 4), named(usual, number - number // 4 - 1))
    mixed = jax.random.permutation(jax.random.fold_in(own, 3), number_of)
    source_of, sink = mixed[0:number_of // 2 * 2:2], mixed[1:number_of // 2 * 2:2]
    room = jnp.minimum(tallies[source_of] - 1, reach - tallies[sink]) // 2
    room = jnp.where((source_of == ranking[0]) | (sink == ranking[0]) | (tallies[sink] == 0), 0, jnp.maximum(room, 0))
    passed = jax.random.randint(jax.random.fold_in(own, 4), (number_of // 2,), 0, 1 << 20) % (room + 1)
    tallies = tallies.at[source_of].add(-passed).at[sink].add(passed)
    items = jnp.searchsorted(jnp.cumsum(tallies), jnp.arange(rows * top), side="right").astype(jnp.int32)
    table = items.reshape(top, rows).T
    table = table[jax.random.permutation(jax.random.fold_in(own, 1), rows)]
    offset_by = jax.random.randint(jax.random.fold_in(own, 2), (rows, 1), 0, top)
    return jnp.take_along_axis(table, (jnp.arange(top)[None, :] + offset_by) % top, axis=1)


def portions_of(count, total, reach, skew, full):
    portions = [(1 << 20) // math.isqrt(rank ** skew) + 1 for rank in range(1, count + 1)]
    largest = reach if full else min(reach, max(-(-total // count), total * portions[0] // sum(portions)))
    least = 1 if total - largest >= count - 1 else 0
    given, surplus = [largest] + [least] * (count - 1), total - largest - least * (count - 1)
    while surplus > 0:
        movable = [i for i in range(1, count) if given[i] < largest] or [i for i in range(1, count) if given[i] < reach]
        whole, remaining = sum([portions[i] for i in movable]), surplus
        for i in movable:
            extra = min(reach - given[i], max(1, remaining * portions[i] // whole), surplus)
            given[i] = given[i] + extra
            surplus = surplus - extra
    return np.array(given)


def normal_values(own_key, shape, width, most, shards=(), kind=jnp.bfloat16):
    result = jax.random.normal(own_key, shape, jnp.float32) * width
    if len(shards) > 0:
        result = levels(own_key, shape, shards, -0.22, 0.18) * result
    return jnp.clip(result, min=-most, max=most).astype(kind)


def setup_inputs(seed: int = 0) -> dict:
    key_list = jax.random.split(jax.random.key(seed), 7)
    a_blocks = normal_values(key_list[0], (ELEMENTS, 7, BLK, BLK), BLK ** -0.5, 0.5, ((0, 256),))
    p_blocks = normal_values(key_list[1], (ELEMENTS, BLK, BLK), BLK ** -0.5, 0.5, ((0, 256),))
    neighbours = touch_ends(jax.random.randint(key_list[2], (ELEMENTS, 6), 0, E_DEV), jax.random.fold_in(key_list[2], 1), 0, E_DEV - 1).astype(jnp.int32)
    coarse_slot = touch_ends(jax.random.randint(key_list[3], (ELEMENTS, 7), 0, KC), jax.random.fold_in(key_list[3], 1), 0, KC - 1).astype(jnp.int32)
    owner_keys = jax.random.split(jax.random.fold_in(key_list[4], 1), ELEMENTS // E_DEV)
    owner_turns = jax.random.permutation(jax.random.fold_in(key_list[4], 3), ELEMENTS // E_DEV)
    owner = jax.vmap(lambda own, number: assign_block(jax.random.fold_in(key_list[4], 2), own, number, E_DEV, OWNERS, 1, CAP, 2))(owner_keys, owner_turns).reshape((ELEMENTS, 1))
    agg_local = touch_ends(jax.random.randint(key_list[5], (ELEMENTS,), 0, AGG_DEV), jax.random.fold_in(key_list[5], 1), 0, AGG_DEV - 1).astype(jnp.int32)
    return {"a_blocks": a_blocks, "p_blocks": p_blocks, "neighbours": neighbours, "coarse_slot": coarse_slot, "owner": owner, "agg_local": agg_local}


def device_terms(a_dev, p_dev, sources, near_dev, slot_dev):
    faces = [p_dev] + [jnp.take(sources[face], near_dev[:, face], axis=0) for face in range(6)]
    facing = jnp.stack(faces, 1)
    applied = jnp.einsum('efik,efkj->efij', a_dev.astype(jnp.float32), facing.astype(jnp.float32)).astype(jnp.bfloat16)
    weighted = jnp.einsum('eki,efkj->efij', p_dev.astype(jnp.float32), applied.astype(jnp.float32))
    onehot = (slot_dev[:, :, None] == jnp.arange(KC, dtype=jnp.int32)[None, None, :]).astype(jnp.float32)
    return jnp.einsum('efs,efij->esij', onehot, weighted, precision=lax.Precision.HIGHEST)


def reference(a_blocks, p_blocks, neighbours, coarse_slot, owner, agg_local):
    p_all = p_blocks.reshape(N_GRP, N_DEV, E_DEV, BLK, BLK)
    padded = jnp.pad(p_all, ((1, 1), (1, 1), (0, 0), (0, 0), (0, 0)))
    a_all = a_blocks.reshape(N_GRP * N_DEV, E_DEV, 7, BLK, BLK)
    near_all = neighbours.reshape(N_GRP * N_DEV, E_DEV, 6)
    slot_all = coarse_slot.reshape(N_GRP * N_DEV, E_DEV, 7)
    owner_all = owner.reshape(N_GRP * N_DEV, E_DEV)
    local_all = agg_local.reshape(N_GRP * N_DEV, E_DEV)
    order = jnp.arange(E_DEV, dtype=jnp.int32)

    def one_device(total, index):
        grp_i = index // N_DEV
        dev_i = index % N_DEV
        p_dev = padded[grp_i + 1, dev_i + 1]
        sources = (p_dev, p_dev, padded[grp_i + 1, dev_i], padded[grp_i + 1, dev_i + 2],
                   padded[grp_i, dev_i + 1], padded[grp_i + 2, dev_i + 1])
        terms = device_terms(a_all[index], p_dev, sources, near_all[index], slot_all[index])
        targets = ((grp_i * N_DEV + owner_all[index]) * AGG_DEV + local_all[index]).astype(jnp.int32)
        same = targets[:, None] == targets[None, :]
        firstidx = jnp.min(jnp.where(same, order[None, :], E_DEV), 1)
        first = (firstidx == order).astype(jnp.float32)
        summed = jnp.einsum('ab,bsij->asij', same.astype(jnp.float32), terms, precision=lax.Precision.HIGHEST)
        rounded = summed.astype(jnp.bfloat16).astype(jnp.float32) * first[:, None, None, None]
        total = total.at[targets].add(rounded)
        return total, None

    start = jnp.zeros((AGGS, KC, BLK, BLK), jnp.float32)
    total, _ = lax.scan(one_device, start, jnp.arange(N_GRP * N_DEV, dtype=jnp.int32))
    return total.astype(jnp.bfloat16)
```

```python
import jax
import jax.numpy as jnp
from jax import lax
from jax.experimental import pallas as pl
from jax.experimental.pallas import tpu as pltpu
from jax.sharding import PartitionSpec as P

KC = 7
NX = 4
NZ = 8
AGG = 8
EB = 4
PIECES = 2
MESH = pl.DeviceIdType.MESH
BF = jnp.bfloat16
F32 = jnp.float32

RELS = (4, 3, 5, 2, 6, 1, 7, 0)
ORDER = tuple(
    (t, p)
    for group in ((0,), (1, 2), (3, 4), (5, 6), (7,))
    for p in range(PIECES)
    for t in group
)
ZOFF = {4: 0, 3: 4, 2: 12, 1: 20}
ZROWS = 28


def halo(p_blocks, axis, up):
    count = lax.axis_size(axis)
    perm = [(i, i + 1) if up else (i + 1, i) for i in range(count - 1)]
    return lax.ppermute(p_blocks, axis, perm)


def rows_kernel(near, slot, pos, a_ref, p_ref, dl_ref, dh_ref, gl_ref, gh_ref, s_hbm, rows, sems):
    step = pl.program_id(0)
    sources = (p_ref, p_ref, dl_ref, dh_ref, gl_ref, gh_ref)
    for j in range(EB):
        e = step * EB + j
        own = p_ref[e]
        faces = [own] + [sources[f][near[e * 6 + f]] for f in range(6)]
        applied = [
            jnp.dot(a_ref[j, f], faces[f], preferred_element_type=F32).astype(BF)
            for f in range(KC)
        ]
        weighted = [
            lax.dot_general(own, w, (((0,), (0,)), ((), ())), preferred_element_type=F32)
            for w in applied
        ]
        for s in range(KC):
            total = None
            for f in range(KC):
                term = jnp.where(slot[e * KC + f] == s, weighted[f], 0.0)
                total = term if total is None else total + term
            rows[e, s] = total.astype(BF)
        pltpu.make_async_copy(rows.at[e], s_hbm.at[pos[e]], sems.at[e]).start()

    @pl.when(step == pl.num_programs(0) - 1)
    def _():
        def finish(e, carry):
            pltpu.make_async_copy(rows.at[e], s_hbm.at[pos[e]], sems.at[e]).wait()
            return carry

        lax.fori_loop(0, rows.shape[0], finish, 0)


def make_rows(a_blocks, p_blocks, low_d, high_d, low_g, high_g, near, slot, pos):
    elems, _, blk, _ = a_blocks.shape
    full = pl.BlockSpec((elems, blk, blk), lambda i, *_: (0, 0, 0), pipeline_mode=pl.Buffered(1))
    return pl.pallas_call(
        rows_kernel,
        grid_spec=pltpu.PrefetchScalarGridSpec(
            num_scalar_prefetch=3,
            grid=(elems // EB,),
            in_specs=[pl.BlockSpec((EB, KC, blk, blk), lambda i, *_: (i, 0, 0, 0))] + [full] * 5,
            out_specs=pl.BlockSpec(memory_space=pl.ANY),
            scratch_shapes=[
                pltpu.VMEM((elems, KC, blk, blk), BF),
                pltpu.SemaphoreType.DMA((elems,)),
            ],
        ),
        out_shape=jax.ShapeDtypeStruct((2 * NX * NZ, KC, blk, blk), BF),
        compiler_params=pltpu.CompilerParams(vmem_limit_bytes=40 << 20),
        name="rows",
    )(near, slot, pos, a_blocks, p_blocks, low_d, high_d, low_g, high_g)


def exchange_kernel(
    labels, s_hbm, out, own, left, right, opp, relay, zs, zr,
    own_sem, x_send, x_recv, z_send, z_recv,
):
    blk = out.shape[2]
    part = blk // PIECES
    g = lax.axis_index("grp")
    d = lax.axis_index("dev")
    z = d // NX
    x = d % NX
    xr = (g, z * NX + (x + 1) % NX)
    xl = (g, z * NX + (x + NX - 1) % NX)
    zu = (g, ((z + 1) % NZ) * NX + x)
    zd = (g, ((z + NZ - 1) % NZ) * NX + x)

    barrier = pltpu.get_barrier_semaphore()
    for peer in (xr, xl, zu, zd):
        pl.semaphore_signal(barrier, inc=1, device_id=peer, device_id_type=MESH)
    pl.semaphore_wait(barrier, 4)

    def base(t, dx):
        return 2 * (((z + RELS[t]) % NZ) * NX + (x + dx) % NX)

    def rows_of(p):
        return pl.ds(p * part, part)

    def remote(kind, t, p, src, dst, peer):
        n = t * PIECES + p
        return pltpu.make_async_remote_copy(
            src_ref=src,
            dst_ref=dst,
            send_sem=x_send.at[kind, n],
            recv_sem=x_recv.at[kind, n],
            device_id=peer,
            device_id_type=MESH,
        )

    def first_hop(t, p):
        r = rows_of(p)
        two = pl.ds(2 * t, 2)
        return (
            remote(0, t, p, s_hbm.at[base(t, 2), :, r], relay.at[2 * t, :, r], xr),
            remote(1, t, p, s_hbm.at[base(t, 2) + 1, :, r], relay.at[2 * t + 1, :, r], xl),
            remote(2, t, p, s_hbm.at[pl.ds(base(t, 1), 2), :, r], left.at[two, :, r], xr),
            remote(3, t, p, s_hbm.at[pl.ds(base(t, 3), 2), :, r], right.at[two, :, r], xl),
        )

    def second_hop(t, p):
        r = rows_of(p)
        return (
            remote(4, t, p, relay.at[2 * t, :, r], opp.at[2 * t, :, r], xr),
            remote(5, t, p, relay.at[2 * t + 1, :, r], opp.at[2 * t + 1, :, r], xl),
        )

    def own_copy(t):
        return pltpu.make_async_copy(
            s_hbm.at[pl.ds(base(t, 0), 2)], own.at[pl.ds(2 * t, 2)], own_sem.at[t]
        )

    def z_copy(way, k, p):
        n = (way * 4 + k - 1) * PIECES + p
        rows = pl.ds(ZOFF[k], 4 if k == 4 else AGG)
        return pltpu.make_async_remote_copy(
            src_ref=zs.at[way, rows, :, rows_of(p)],
            dst_ref=zr.at[way, rows, :, rows_of(p)],
            send_sem=z_send.at[n],
            recv_sem=z_recv.at[n],
            device_id=zu if way == 0 else zd,
            device_id_type=MESH,
        )

    def combine(t, p, first, count, arrived, put):
        r = rows_of(p)
        names = [
            labels[src * 2 * NX * NZ + base(t, 0) + k] for src in range(4) for k in range(2)
        ]

        def one(i, carry):
            a = first + i
            picks = [name == a for name in names]

            def slot(s, inner):
                total = None
                for ref in arrived:
                    term = ref(i, s).astype(F32)
                    total = term if total is None else total + term
                n = 0
                for ref in (own, left, right, opp):
                    for k in range(2):
                        term = jnp.where(picks[n], ref[2 * t + k, s, r].astype(F32), 0.0)
                        total = term if total is None else total + term
                        n += 1
                put(i, s, total.astype(BF))
                return inner

            return lax.fori_loop(0, KC, slot, carry)

        lax.fori_loop(0, count, one, 0)

    def from_z(way, row, p):
        return lambda i, s: zr[way, row + i, s, rows_of(p)]

    def to_z(way, row, p):
        def put(i, s, value):
            zs[way, row + i, s, rows_of(p)] = value

        return put

    def step(t, p):
        rel = RELS[t]
        if rel == 4:
            combine(t, p, 0, 4, (), to_z(0, 0, p))
            z_copy(0, 4, p).start()
            combine(t, p, 4, 4, (), to_z(1, 0, p))
            z_copy(1, 4, p).start()
        elif rel == 0:
            for way in range(2):
                z_copy(way, 1, p).wait_recv()

            def put(i, s, value):
                out[i, s, rows_of(p)] = value

            combine(t, p, 0, AGG, (from_z(0, ZOFF[1], p), from_z(1, ZOFF[1], p)), put)
        else:
            way, k = (0, rel) if rel < 4 else (1, NZ - rel)
            z_copy(way, k + 1, p).wait_recv()
            if k == 3:
                lower = (from_z(0, 0, p),) if way == 0 else ()
                upper = (from_z(1, 0, p),) if way == 1 else ()
                combine(t, p, 0, 4, lower, to_z(way, ZOFF[3], p))
                combine(t, p, 4, 4, upper, to_z(way, ZOFF[3] + 4, p))
            else:
                combine(t, p, 0, AGG, (from_z(way, ZOFF[k + 1], p),), to_z(way, ZOFF[k], p))
            z_copy(way, k, p).start()

    for copy in first_hop(*ORDER[0]):
        copy.start()
    for t in range(NZ):
        own_copy(t).start()
    for n, (t, p) in enumerate(ORDER):
        hop = first_hop(t, p)
        again = second_hop(t, p)
        for way in range(2):
            hop[way].wait_recv()
            again[way].start()
        if n + 1 < len(ORDER):
            for copy in first_hop(*ORDER[n + 1]):
                copy.start()
        if p == 0:
            own_copy(t).wait()
        hop[2].wait_recv()
        hop[3].wait_recv()
        again[0].wait_recv()
        again[1].wait_recv()
        step(t, p)
    for t, p in ORDER:
        for copy in first_hop(t, p) + second_hop(t, p):
            copy.wait_send()
    for way in range(2):
        for k in range(1, 5):
            for p in range(PIECES):
                z_copy(way, k, p).wait_send()


def exchange(labels, rows):
    _, _, blk, _ = rows.shape
    block = (KC, blk, blk)
    n = NZ * PIECES
    return pl.pallas_call(
        exchange_kernel,
        in_specs=[
            pl.BlockSpec(memory_space=pltpu.SMEM),
            pl.BlockSpec(memory_space=pl.ANY),
        ],
        out_specs=pl.BlockSpec(memory_space=pltpu.VMEM),
        out_shape=jax.ShapeDtypeStruct((AGG,) + block, BF),
        scratch_shapes=[
            pltpu.VMEM((2 * NZ,) + block, BF),
            pltpu.VMEM((2 * NZ,) + block, BF),
            pltpu.VMEM((2 * NZ,) + block, BF),
            pltpu.VMEM((2 * NZ,) + block, BF),
            pltpu.VMEM((2 * NZ,) + block, BF),
            pltpu.VMEM((2, ZROWS) + block, BF),
            pltpu.VMEM((2, ZROWS) + block, BF),
            pltpu.SemaphoreType.DMA((NZ,)),
            pltpu.SemaphoreType.DMA((6, n)),
            pltpu.SemaphoreType.DMA((6, n)),
            pltpu.SemaphoreType.DMA((n,)),
            pltpu.SemaphoreType.DMA((n,)),
        ],
        compiler_params=pltpu.CompilerParams(
            collective_id=0, has_side_effects=True, vmem_limit_bytes=58 << 20
        ),
        name="exchange",
    )(labels, rows)


def on_device(a_blocks, p_blocks, neighbours, coarse_slot, owner, agg_local):
    elems = p_blocks.shape[0]
    low_d, high_d = halo(p_blocks, "dev", True), halo(p_blocks, "dev", False)
    low_g, high_g = halo(p_blocks, "grp", True), halo(p_blocks, "grp", False)
    targets = owner[:, 0]
    order = jnp.arange(elems, dtype=jnp.int32)
    earlier = (targets[:, None] == targets[None, :]) & (order[None, :] < order[:, None])
    pos = 2 * targets + jnp.sum(earlier.astype(jnp.int32), 1)
    holds = jnp.arange(2 * NX * NZ, dtype=jnp.int32)[:, None] == pos[None, :]
    labels = jnp.sum(jnp.where(holds, agg_local[None, :] + 1, 0), 1) - 1

    def from_x(step):
        perm = [
            (z * NX + x, z * NX + (x + step) % NX) for z in range(NZ) for x in range(NX)
        ]
        return lax.ppermute(labels, "dev", perm)

    all_labels = jnp.concatenate([labels, from_x(1), from_x(NX - 1), from_x(2)])
    rows = make_rows(
        a_blocks, p_blocks, low_d, high_d, low_g, high_g,
        neighbours.reshape(-1), coarse_slot.reshape(-1), pos,
    )
    return exchange(all_labels, rows)


def solution(mesh):
    placed = (
        P(("grp", "dev"), None, None, None),
        P(("grp", "dev"), None, None),
        P(("grp", "dev"), None),
        P(("grp", "dev"), None),
        P(("grp", "dev"), None),
        P(("grp", "dev")),
    )
    return jax.shard_map(
        on_device,
        mesh=mesh,
        in_specs=placed,
        out_specs=P(("grp", "dev"), None, None, None),
        check_vma=False,
    )
```

```python
import jax
import jax.numpy as jnp
from jax import lax
from jax.experimental import pallas as pl
from jax.experimental.pallas import tpu as pltpu
from jax.sharding import PartitionSpec as P

KC = 7
NX = 4
NZ = 8
AGG = 8
SLOTS = 2 * NX * NZ
PIECES = 2
RING = 4
MESH = pl.DeviceIdType.MESH
BF = jnp.bfloat16
F32 = jnp.float32
I32 = jnp.int32

RELS = (4, 3, 5, 2, 6, 1, 7, 0)
ORDER = tuple(
    (t, p)
    for group in ((0,), (1, 2), (3, 4), (5, 6), (7,))
    for p in range(PIECES)
    for t in group
)
ZIN = {4: 0, 3: 4, 2: 12, 1: 20}
ZIN_ROWS = 28
ZOUT = {4: 0, 3: 4, 2: 12, 1: 4}
ZOUT_ROWS = 20
SOURCE = (0, 0, 0, 1, 2, 3, 4)


def tables_kernel(owner, agg_local, elem, label, used):
    def clear(i, carry):
        elem[i] = 0
        label[0, i] = -1
        return carry

    def clear_used(i, carry):
        used[i] = 0
        return carry

    def place(e, carry):
        o = owner[0, e]
        r = 2 * o + used[o]
        used[o] = used[o] + 1
        elem[r] = e
        label[0, r] = agg_local[0, e]
        return carry

    lax.fori_loop(0, SLOTS, clear, 0)
    lax.fori_loop(0, SLOTS // 2, clear_used, 0)
    lax.fori_loop(0, owner.shape[1], place, 0)


def make_tables(owner, agg_local):
    smem = pl.BlockSpec(memory_space=pltpu.SMEM)
    return pl.pallas_call(
        tables_kernel,
        in_specs=[smem, smem],
        out_specs=[smem, smem],
        out_shape=[
            jax.ShapeDtypeStruct((SLOTS,), I32),
            jax.ShapeDtypeStruct((8, 128), I32),
        ],
        scratch_shapes=[pltpu.SMEM((SLOTS // 2,), I32)],
        name="tables",
    )(owner, agg_local)


def coarse_kernel(
    elem, near, slot, label, a_hbm, p_hbm, out,
    av, pv, sv, left, right, opp, relay, zs, zr, lv, names,
    in_sem, halo_send, halo_recv, lab_send, lab_recv, lab_sem, x_send, x_recv, z_send, z_recv,
):
    elems, blk, _ = p_hbm.shape
    part = blk // PIECES
    ng, nd = lax.axis_size("grp"), lax.axis_size("dev")
    g = lax.axis_index("grp")
    d = lax.axis_index("dev")
    z = d // NX
    x = d % NX
    xr = (g, z * NX + (x + 1) % NX)
    xl = (g, z * NX + (x + NX - 1) % NX)
    xo = (g, z * NX + (x + 2) % NX)
    zu = (g, ((z + 1) % NZ) * NX + x)
    zd = (g, ((z + NZ - 1) % NZ) * NX + x)

    halos = (
        (d < nd - 1, (g, (d + 1) % nd), d > 0),
        (d > 0, (g, (d + nd - 1) % nd), d < nd - 1),
        (g < ng - 1, ((g + 1) % ng, d), g > 0),
        (g > 0, ((g + ng - 1) % ng, d), g < ng - 1),
    )

    load_p = pltpu.make_async_copy(p_hbm, pv.at[0], in_sem.at[0])
    load_a = pltpu.make_async_copy(a_hbm, av, in_sem.at[1])
    load_p.start()
    load_a.start()

    barrier = pltpu.get_barrier_semaphore()
    expected = 5
    for peer in (xr, xl, xo, zu, zd):
        pl.semaphore_signal(barrier, inc=1, device_id=peer, device_id_type=MESH)
    for sends, peer, gets in halos:
        @pl.when(sends)
        def _():
            pl.semaphore_signal(barrier, inc=1, device_id=peer, device_id_type=MESH)

        expected = expected + jnp.where(gets, 1, 0)
    pl.semaphore_wait(barrier, expected)

    def halo_copy(i):
        return pltpu.make_async_remote_copy(
            src_ref=p_hbm,
            dst_ref=pv.at[1 + i],
            send_sem=halo_send.at[i],
            recv_sem=halo_recv.at[i],
            device_id=halos[i][1],
            device_id_type=MESH,
        )

    for i in range(4):
        @pl.when(halos[i][0])
        def _():
            halo_copy(i).start()

    def label_copy(i):
        return pltpu.make_async_remote_copy(
            src_ref=label,
            dst_ref=lv.at[1 + i],
            send_sem=lab_send.at[i],
            recv_sem=lab_recv.at[i],
            device_id=(xr, xl, xo)[i],
            device_id_type=MESH,
        )

    for i in range(3):
        label_copy(i).start()
    lv[0] = label[...]

    for i in range(4):
        @pl.when(jnp.logical_not(halos[i][2]))
        def _():
            def clear(e, carry):
                pv[1 + i, e] = jnp.zeros((blk, blk), BF)
                return carry

            lax.fori_loop(0, elems, clear, 0)

    for i in range(3):
        label_copy(i).wait_recv()
    load_names = pltpu.make_async_copy(lv, names, lab_sem.at[0])
    load_names.start()
    load_p.wait()
    load_a.wait()
    for i in (2, 3, 0, 1):
        @pl.when(halos[i][2])
        def _():
            halo_copy(i).wait_recv()

    def base(t, dx):
        return 2 * (((z + RELS[t]) % NZ) * NX + (x + dx) % NX)

    def compute(t, dx):
        for k in range(2):
            e = elem[base(t, dx) + k]
            own = pv[0, e]
            weighted = []
            for f in range(KC):
                face = own if f == 0 else pv[SOURCE[f], near[f - 1, e]]
                applied = jnp.dot(av[e, f], face, preferred_element_type=F32).astype(BF)
                weighted.append(
                    lax.dot_general(
                        own, applied, (((0,), (0,)), ((), ())), preferred_element_type=F32
                    )
                )
            for s in range(KC):
                total = None
                for f in range(KC):
                    term = jnp.where(slot[f, e] == s, weighted[f], 0.0)
                    total = term if total is None else total + term
                sv[(t % RING) * 8 + 2 * dx + k, s] = total.astype(BF)

    def compute_all(t):
        def one(dx, carry):
            compute(t, dx)
            return carry

        lax.fori_loop(0, NX, one, 0)

    def rows_of(p):
        return pl.ds(p * part, part)

    def remote(kind, t, p, src, dst, peer):
        n = t * PIECES + p
        return pltpu.make_async_remote_copy(
            src_ref=src,
            dst_ref=dst,
            send_sem=x_send.at[kind, n],
            recv_sem=x_recv.at[kind, n],
            device_id=peer,
            device_id_type=MESH,
        )

    def first_hop(t, p):
        r = rows_of(p)
        two = pl.ds(2 * t, 2)
        q = (t % RING) * 8
        return (
            remote(0, t, p, sv.at[q + 4, :, r], relay.at[2 * t, :, r], xr),
            remote(1, t, p, sv.at[q + 5, :, r], relay.at[2 * t + 1, :, r], xl),
            remote(2, t, p, sv.at[pl.ds(q + 2, 2), :, r], left.at[two, :, r], xr),
            remote(3, t, p, sv.at[pl.ds(q + 6, 2), :, r], right.at[two, :, r], xl),
        )

    def second_hop(t, p):
        r = rows_of(p)
        return (
            remote(4, t, p, relay.at[2 * t, :, r], opp.at[2 * t, :, r], xr),
            remote(5, t, p, relay.at[2 * t + 1, :, r], opp.at[2 * t + 1, :, r], xl),
        )

    def z_copy(way, k, p):
        n = (way * 4 + k - 1) * PIECES + p
        count = 4 if k == 4 else AGG
        return pltpu.make_async_remote_copy(
            src_ref=zs.at[way, pl.ds(ZOUT[k], count), :, rows_of(p)],
            dst_ref=zr.at[way, pl.ds(ZIN[k], count), :, rows_of(p)],
            send_sem=z_send.at[n],
            recv_sem=z_recv.at[n],
            device_id=zu if way == 0 else zd,
            device_id_type=MESH,
        )

    def combine(t, p, first, count, arrived, put):
        r = rows_of(p)
        own_of = [names[src, 0, base(t, 0) + k] for src in range(4) for k in range(2)]
        rows = [(sv, (t % RING) * 8), (left, 2 * t), (right, 2 * t), (opp, 2 * t)]

        def one(i, carry):
            a = first + i
            picks = [name == a for name in own_of]

            def block(s, inner):
                total = None
                for ref in arrived:
                    term = ref(i, s).astype(F32)
                    total = term if total is None else total + term
                n = 0
                for ref, q in rows:
                    for k in range(2):
                        term = jnp.where(picks[n], ref[q + k, s, r].astype(F32), 0.0)
                        total = term if total is None else total + term
                        n += 1
                put(i, s, total.astype(BF))
                return inner

            return lax.fori_loop(0, KC, block, carry)

        lax.fori_loop(0, count, one, 0)

    def from_z(way, row, p):
        return lambda i, s: zr[way, row + i, s, rows_of(p)]

    def to_z(way, row, p):
        def put(i, s, value):
            zs[way, row + i, s, rows_of(p)] = value

        return put

    def step(t, p):
        rel = RELS[t]
        if rel == 4:
            for way in range(2):
                combine(t, p, 4 * way, 4, (), to_z(way, ZOUT[4], p))
                z_copy(way, 4, p).start()
        elif rel == 0:
            for way in range(2):
                z_copy(way, 1, p).wait_recv()

            def put(i, s, value):
                out[i, s, rows_of(p)] = value

            combine(t, p, 0, AGG, (from_z(0, ZIN[1], p), from_z(1, ZIN[1], p)), put)
        else:
            way, k = (0, rel) if rel < 4 else (1, NZ - rel)
            if k == 1:
                z_copy(way, 3, p).wait_send()
            z_copy(way, k + 1, p).wait_recv()
            if k == 3:
                for half in range(2):
                    arrived = (from_z(way, ZIN[4], p),) if half == way else ()
                    combine(t, p, 4 * half, 4, arrived, to_z(way, ZOUT[3] + 4 * half, p))
            else:
                combine(t, p, 0, AGG, (from_z(way, ZIN[k + 1], p),), to_z(way, ZOUT[k], p))
            z_copy(way, k, p).start()

    start_t, start_p = ORDER[0]
    hop = first_hop(start_t, start_p)
    compute(start_t, 2)
    hop[0].start()
    hop[1].start()
    compute(start_t, 1)
    hop[2].start()
    compute(start_t, 3)
    hop[3].start()
    compute(start_t, 0)
    load_names.wait()
    done = {start_t}
    for n, (t, p) in enumerate(ORDER):
        hop = first_hop(t, p)
        again = second_hop(t, p)
        for way in range(2):
            hop[way].wait_recv()
            again[way].start()
        if n + 1 < len(ORDER):
            for copy in first_hop(*ORDER[n + 1]):
                copy.start()
        if n + 2 < len(ORDER) and ORDER[n + 2][0] not in done:
            later = ORDER[n + 2][0]
            done.add(later)
            if later >= RING:
                for q in range(PIECES):
                    for copy in first_hop(later - RING, q):
                        copy.wait_send()
            compute_all(later)
        hop[2].wait_recv()
        hop[3].wait_recv()
        again[0].wait_recv()
        again[1].wait_recv()
        step(t, p)
    for t, p in ORDER:
        copies = second_hop(t, p)
        if t + RING >= NZ:
            copies = copies + first_hop(t, p)
        for copy in copies:
            copy.wait_send()
    for way in range(2):
        for k in (1, 2, 4):
            for p in range(PIECES):
                z_copy(way, k, p).wait_send()
    for i in range(3):
        label_copy(i).wait_send()
    for i in range(4):
        @pl.when(halos[i][0])
        def _():
            halo_copy(i).wait_send()


def make_coarse(elem, near, slot, label, a_blocks, p_blocks):
    elems, blk, _ = p_blocks.shape
    block = (KC, blk, blk)
    n = NZ * PIECES
    smem = pl.BlockSpec(memory_space=pltpu.SMEM)
    hbm = pl.BlockSpec(memory_space=pl.ANY)
    dma = pltpu.SemaphoreType.DMA
    return pl.pallas_call(
        coarse_kernel,
        in_specs=[smem, smem, smem, pl.BlockSpec(memory_space=pltpu.VMEM), hbm, hbm],
        out_specs=pl.BlockSpec(memory_space=pltpu.VMEM),
        out_shape=jax.ShapeDtypeStruct((AGG,) + block, BF),
        scratch_shapes=[
            pltpu.VMEM((elems,) + block, BF),
            pltpu.VMEM((5, elems, blk, blk), BF),
            pltpu.VMEM((8 * RING,) + block, BF),
            pltpu.VMEM((2 * NZ,) + block, BF),
            pltpu.VMEM((2 * NZ,) + block, BF),
            pltpu.VMEM((2 * NZ,) + block, BF),
            pltpu.VMEM((2 * NZ,) + block, BF),
            pltpu.VMEM((2, ZOUT_ROWS) + block, BF),
            pltpu.VMEM((2, ZIN_ROWS) + block, BF),
            pltpu.VMEM((4, 8, 128), I32),
            pltpu.SMEM((4, 8, 128), I32),
            dma((2,)),
            dma((4,)),
            dma((4,)),
            dma((3,)),
            dma((3,)),
            dma((1,)),
            dma((6, n)),
            dma((6, n)),
            dma((n,)),
            dma((n,)),
        ],
        compiler_params=pltpu.CompilerParams(
            collective_id=0, has_side_effects=True, vmem_limit_bytes=63 << 20
        ),
        name="coarse",
    )(elem, near, slot, label, a_blocks, p_blocks)


def on_device(a_blocks, p_blocks, neighbours, coarse_slot, owner, agg_local):
    elem, label = make_tables(owner.T, agg_local[None, :])
    return make_coarse(elem, neighbours.T, coarse_slot.T, label, a_blocks, p_blocks)


def solution(mesh):
    placed = (
        P(("grp", "dev"), None, None, None),
        P(("grp", "dev"), None, None),
        P(("grp", "dev"), None),
        P(("grp", "dev"), None),
        P(("grp", "dev"), None),
        P(("grp", "dev")),
    )
    return jax.shard_map(
        on_device,
        mesh=mesh,
        in_specs=placed,
        out_specs=P(("grp", "dev"), None, None, None),
        check_vma=False,
    )
```

```python
import jax
import jax.numpy as jnp
from jax import lax
from jax.experimental import pallas as pl
from jax.experimental.pallas import tpu as pltpu
from jax.sharding import PartitionSpec as P

KC = 7
NX = 4
NZ = 8
AGG = 8
SLOTS = 2 * NX * NZ
PIECES = 2
RING = 4
MESH = pl.DeviceIdType.MESH
BF = jnp.bfloat16
F32 = jnp.float32
I32 = jnp.int32

RELS = (4, 3, 5, 2, 6, 1, 7, 0)
ORDER = tuple(
    (t, p)
    for group in ((0,), (1, 2), (3, 4), (5, 6), (7,))
    for p in range(PIECES)
    for t in group
)
ZIN = {4: 0, 3: 4, 2: 12, 1: 20}
ZIN_ROWS = 28
ZOUT = {4: 0, 3: 4, 2: 12, 1: 4}
ZOUT_ROWS = 20
SOURCE = (0, 0, 0, 1, 2, 3, 4)


def coarse_kernel(
    owner, agg_local, near, slot, a_hbm, p_hbm, out,
    av, pv, sv, left, right, opp, relay, zs, zr, result, lv, names, elem, twin, label,
    in_sem, out_sem, halo_send, halo_recv, lab_send, lab_recv, lab_sem, x_send, x_recv, z_send, z_recv,
):
    elems, blk, _ = p_hbm.shape
    part = blk // PIECES
    ng, nd = lax.axis_size("grp"), lax.axis_size("dev")
    g = lax.axis_index("grp")
    d = lax.axis_index("dev")
    z = d // NX
    x = d % NX
    xr = (g, z * NX + (x + 1) % NX)
    xl = (g, z * NX + (x + NX - 1) % NX)
    xo = (g, z * NX + (x + 2) % NX)
    sense = 1 + (NZ - 2) * (g % 2)
    zu = (g, ((z + sense) % NZ) * NX + x)
    zd = (g, ((z + NZ - sense) % NZ) * NX + x)

    halos = (
        (d < nd - 1, (g, (d + 1) % nd), d > 0),
        (d > 0, (g, (d + nd - 1) % nd), d < nd - 1),
        (g < ng - 1, ((g + 1) % ng, d), g > 0),
        (g > 0, ((g + ng - 1) % ng, d), g < ng - 1),
    )

    load_p = pltpu.make_async_copy(p_hbm, pv.at[0], in_sem.at[0])
    load_a = pltpu.make_async_copy(a_hbm, av, in_sem.at[1])
    load_p.start()
    load_a.start()

    barrier = pltpu.get_barrier_semaphore()
    expected = 5
    for peer in (xr, xl, xo, zu, zd):
        pl.semaphore_signal(barrier, inc=1, device_id=peer, device_id_type=MESH)
    for sends, peer, gets in halos:
        @pl.when(sends)
        def _():
            pl.semaphore_signal(barrier, inc=1, device_id=peer, device_id_type=MESH)

        expected = expected + jnp.where(gets, 1, 0)
    pl.semaphore_wait(barrier, expected)

    def halo_copy(i):
        return pltpu.make_async_remote_copy(
            src_ref=p_hbm,
            dst_ref=pv.at[1 + i],
            send_sem=halo_send.at[i],
            recv_sem=halo_recv.at[i],
            device_id=halos[i][1],
            device_id_type=MESH,
        )

    for i in range(4):
        @pl.when(halos[i][0])
        def _():
            halo_copy(i).start()

    def label_copy(i):
        return pltpu.make_async_remote_copy(
            src_ref=lv.at[0],
            dst_ref=lv.at[1 + i],
            send_sem=lab_send.at[i],
            recv_sem=lab_recv.at[i],
            device_id=(xr, xl, xo)[i],
            device_id_type=MESH,
        )

    def place(o, carry):
        one, two = -1, -1
        for i in range(elems):
            e = elems - 1 - i
            here = owner[0, e] == o
            two = jnp.where(here, one, two)
            one = jnp.where(here, e, one)
        first, second = jnp.maximum(one, 0), jnp.maximum(two, 0)
        name = jnp.where(one < 0, -1, agg_local[0, first])
        other = jnp.where(two < 0, -1, agg_local[0, second])
        same = jnp.logical_and(two >= 0, name == other)
        elem[2 * o] = first
        elem[2 * o + 1] = second
        twin[o] = jnp.where(same, 1, 0)
        label[0, 2 * o] = name
        label[0, 2 * o + 1] = jnp.where(same, -1, other)
        return carry

    lax.fori_loop(0, SLOTS // 2, place, 0)
    share = pltpu.make_async_copy(label, lv.at[0], lab_sem.at[1])
    share.start()
    share.wait()
    for i in range(3):
        label_copy(i).start()

    for i in range(4):
        @pl.when(jnp.logical_not(halos[i][2]))
        def _():
            def clear(e, carry):
                pv[1 + i, e] = jnp.zeros((blk, blk), BF)
                return carry

            lax.fori_loop(0, elems, clear, 0)

    for i in range(3):
        label_copy(i).wait_recv()
    load_names = pltpu.make_async_copy(lv, names, lab_sem.at[0])
    load_names.start()
    load_p.wait()
    load_a.wait()
    for i in (2, 3, 0, 1):
        @pl.when(halos[i][2])
        def _():
            halo_copy(i).wait_recv()

    def base(t, dx):
        return 2 * (((z + sense * RELS[t]) % NZ) * NX + (x + dx) % NX)

    def compute(t, dx):
        for k in (1, 0):
            e = elem[base(t, dx) + k]
            own = pv[0, e]
            weighted = []
            for f in range(KC):
                face = own if f == 0 else pv[SOURCE[f], near[f - 1, e]]
                applied = jnp.dot(av[e, f], face, preferred_element_type=F32).astype(BF)
                weighted.append(
                    lax.dot_general(
                        own, applied, (((0,), (0,)), ((), ())), preferred_element_type=F32
                    )
                )
            for s in range(KC):
                total = None
                for f in range(KC):
                    term = jnp.where(slot[f, e] == s, weighted[f], 0.0)
                    total = term if total is None else total + term
                row = (t % RING) * 8 + 2 * dx
                if k == 0:
                    second = sv[row + 1, s].astype(F32)
                    total = total + jnp.where(twin[base(t, dx) // 2] == 1, second, 0.0)
                sv[row + k, s] = total.astype(BF)

    def compute_all(t):
        def one(dx, carry):
            compute(t, dx)
            return carry

        lax.fori_loop(0, NX, one, 0)

    def rows_of(p):
        return pl.ds(p * part, part)

    def remote(kind, t, p, src, dst, peer):
        n = t * PIECES + p
        return pltpu.make_async_remote_copy(
            src_ref=src,
            dst_ref=dst,
            send_sem=x_send.at[kind, n],
            recv_sem=x_recv.at[kind, n],
            device_id=peer,
            device_id_type=MESH,
        )

    def first_hop(t, p):
        r = rows_of(p)
        two = pl.ds(2 * t, 2)
        q = (t % RING) * 8
        return (
            remote(0, t, p, sv.at[q + 4, :, r], relay.at[2 * t, :, r], xr),
            remote(1, t, p, sv.at[q + 5, :, r], relay.at[2 * t + 1, :, r], xl),
            remote(2, t, p, sv.at[pl.ds(q + 2, 2), :, r], left.at[two, :, r], xr),
            remote(3, t, p, sv.at[pl.ds(q + 6, 2), :, r], right.at[two, :, r], xl),
        )

    def second_hop(t, p):
        r = rows_of(p)
        return (
            remote(4, t, p, relay.at[2 * t, :, r], opp.at[2 * t, :, r], xr),
            remote(5, t, p, relay.at[2 * t + 1, :, r], opp.at[2 * t + 1, :, r], xl),
        )

    def z_copy(way, k, p):
        n = (way * 4 + k - 1) * PIECES + p
        count = 4 if k == 4 else AGG
        return pltpu.make_async_remote_copy(
            src_ref=zs.at[way, pl.ds(ZOUT[k], count), :, rows_of(p)],
            dst_ref=zr.at[way, pl.ds(ZIN[k], count), :, rows_of(p)],
            send_sem=z_send.at[n],
            recv_sem=z_recv.at[n],
            device_id=zu if way == 0 else zd,
            device_id_type=MESH,
        )

    def combine(t, p, first, count, arrived, put):
        r = rows_of(p)
        own_of = [names[src, 0, base(t, 0) + k] for src in range(4) for k in range(2)]
        rows = [(sv, (t % RING) * 8), (left, 2 * t), (right, 2 * t), (opp, 2 * t)]

        def one(i, carry):
            a = first + i
            picks = [name == a for name in own_of]

            def block(s, inner):
                total = None
                for ref in arrived:
                    term = ref(i, s).astype(F32)
                    total = term if total is None else total + term
                nothing = jnp.zeros((part, blk), BF)
                for n, (ref, q) in enumerate(rows):
                    term = lax.select(picks[2 * n + 1], ref[q + 1, s, r], nothing)
                    term = lax.select(picks[2 * n], ref[q, s, r], term).astype(F32)
                    total = term if total is None else total + term
                put(i, s, total.astype(BF))
                return inner

            return lax.fori_loop(0, KC, block, carry)

        lax.fori_loop(0, count, one, 0)

    def from_z(way, row, p):
        return lambda i, s: zr[way, row + i, s, rows_of(p)]

    def to_z(way, row, p):
        def put(i, s, value):
            zs[way, row + i, s, rows_of(p)] = value

        return put

    def out_copy(p):
        return pltpu.make_async_copy(
            result.at[:, :, rows_of(p)], out.at[:, :, rows_of(p)], out_sem.at[p]
        )

    def step(t, p):
        rel = RELS[t]
        if rel == 4:
            for way in range(2):
                combine(t, p, 4 * way, 4, (), to_z(way, ZOUT[4], p))
                z_copy(way, 4, p).start()
        elif rel == 0:
            for way in range(2):
                z_copy(way, 1, p).wait_recv()

            def put(i, s, value):
                result[i, s, rows_of(p)] = value

            combine(t, p, 0, AGG, (from_z(0, ZIN[1], p), from_z(1, ZIN[1], p)), put)
            out_copy(p).start()
        else:
            way, k = (0, rel) if rel < 4 else (1, NZ - rel)
            if k == 1:
                z_copy(way, 3, p).wait_send()
            z_copy(way, k + 1, p).wait_recv()
            if k == 3:
                for half in range(2):
                    arrived = (from_z(way, ZIN[4], p),) if half == way else ()
                    combine(t, p, 4 * half, 4, arrived, to_z(way, ZOUT[3] + 4 * half, p))
            else:
                combine(t, p, 0, AGG, (from_z(way, ZIN[k + 1], p),), to_z(way, ZOUT[k], p))
            z_copy(way, k, p).start()

    start_t, start_p = ORDER[0]
    hop = first_hop(start_t, start_p)
    compute(start_t, 2)
    hop[0].start()
    hop[1].start()
    compute(start_t, 1)
    hop[2].start()
    compute(start_t, 3)
    hop[3].start()
    compute(start_t, 0)
    load_names.wait()
    done = {start_t}
    for n, (t, p) in enumerate(ORDER):
        hop = first_hop(t, p)
        again = second_hop(t, p)
        for way in range(2):
            hop[way].wait_recv()
            again[way].start()
        if n + 1 < len(ORDER):
            for copy in first_hop(*ORDER[n + 1]):
                copy.start()
        if n + 2 < len(ORDER) and ORDER[n + 2][0] not in done:
            later = ORDER[n + 2][0]
            done.add(later)
            if later >= RING:
                for q in range(PIECES):
                    for copy in first_hop(later - RING, q):
                        copy.wait_send()
            compute_all(later)
        hop[2].wait_recv()
        hop[3].wait_recv()
        again[0].wait_recv()
        again[1].wait_recv()
        step(t, p)
    for t, p in ORDER:
        copies = second_hop(t, p)
        if t + RING >= NZ:
            copies = copies + first_hop(t, p)
        for copy in copies:
            copy.wait_send()
    for way in range(2):
        for k in (1, 2, 4):
            for p in range(PIECES):
                z_copy(way, k, p).wait_send()
    for i in range(3):
        label_copy(i).wait_send()
    for p in range(PIECES):
        out_copy(p).wait()
    for i in range(4):
        @pl.when(halos[i][0])
        def _():
            halo_copy(i).wait_send()


def make_coarse(owner, agg_local, near, slot, a_blocks, p_blocks):
    elems, blk, _ = p_blocks.shape
    block = (KC, blk, blk)
    n = NZ * PIECES
    smem = pl.BlockSpec(memory_space=pltpu.SMEM)
    hbm = pl.BlockSpec(memory_space=pl.ANY)
    dma = pltpu.SemaphoreType.DMA
    return pl.pallas_call(
        coarse_kernel,
        in_specs=[smem, smem, smem, smem, hbm, hbm],
        out_specs=hbm,
        out_shape=jax.ShapeDtypeStruct((AGG,) + block, BF),
        scratch_shapes=[
            pltpu.VMEM((elems,) + block, BF),
            pltpu.VMEM((5, elems, blk, blk), BF),
            pltpu.VMEM((8 * RING,) + block, BF),
            pltpu.VMEM((2 * NZ,) + block, BF),
            pltpu.VMEM((2 * NZ,) + block, BF),
            pltpu.VMEM((2 * NZ,) + block, BF),
            pltpu.VMEM((2 * NZ,) + block, BF),
            pltpu.VMEM((2, ZOUT_ROWS) + block, BF),
            pltpu.VMEM((2, ZIN_ROWS) + block, BF),
            pltpu.VMEM((AGG,) + block, BF),
            pltpu.VMEM((4, 8, 128), I32),
            pltpu.SMEM((4, 8, 128), I32),
            pltpu.SMEM((SLOTS,), I32),
            pltpu.SMEM((SLOTS // 2,), I32),
            pltpu.SMEM((8, 128), I32),
            dma((2,)),
            dma((PIECES,)),
            dma((4,)),
            dma((4,)),
            dma((3,)),
            dma((3,)),
            dma((2,)),
            dma((6, n)),
            dma((6, n)),
            dma((n,)),
            dma((n,)),
        ],
        compiler_params=pltpu.CompilerParams(
            collective_id=0, has_side_effects=True, vmem_limit_bytes=60 << 20
        ),
        name="coarse",
    )(owner, agg_local, near, slot, a_blocks, p_blocks)


def on_device(a_blocks, p_blocks, neighbours, coarse_slot, owner, agg_local):
    return make_coarse(
        owner.T, agg_local[None, :], neighbours.T, coarse_slot.T, a_blocks, p_blocks
    )


def solution(mesh):
    placed = (
        P(("grp", "dev"), None, None, None),
        P(("grp", "dev"), None, None),
        P(("grp", "dev"), None),
        P(("grp", "dev"), None),
        P(("grp", "dev"), None),
        P(("grp", "dev")),
    )
    return jax.shard_map(
        on_device,
        mesh=mesh,
        in_specs=placed,
        out_specs=P(("grp", "dev"), None, None, None),
        check_vma=False,
    )
```

```python
import jax
import jax.numpy as jnp
from jax import lax
from jax.experimental import pallas as pl
from jax.experimental.pallas import tpu as pltpu
from jax.sharding import PartitionSpec as P

KC = 7
NX = 4
NZ = 8
AGG = 8
SLOTS = 2 * NX * NZ
SPLIT = ((0, 4), (4, 3))
PIECES = len(SPLIT)
RING = 4
MESH = pl.DeviceIdType.MESH
BF = jnp.bfloat16
F32 = jnp.float32
I32 = jnp.int32

RELS = (4, 3, 5, 2, 6, 1, 7, 0)
ORDER = tuple(
    (t, p)
    for group in ((0,), (1, 2), (3, 4), (5, 6), (7,))
    for p in range(PIECES)
    for t in group
)
ZIN = {4: 0, 3: 4, 2: 12, 1: 20}
ZIN_ROWS = 28
ZOUT = {4: 0, 3: 4, 2: 12, 1: 4}
ZOUT_ROWS = 20
SOURCE = (0, 0, 0, 1, 2, 3, 4)


def coarse_kernel(
    owner, agg_local, near, slot, a_hbm, p_hbm, out,
    av, pv, sv, left, right, opp, relay, zs, zr, lv, names, elem, twin, label,
    in_sem, halo_send, halo_recv, lab_send, lab_recv, lab_sem, x_send, x_recv, z_send, z_recv,
):
    elems, blk, _ = p_hbm.shape
    ng, nd = lax.axis_size("grp"), lax.axis_size("dev")
    g = lax.axis_index("grp")
    d = lax.axis_index("dev")
    z = d // NX
    x = d % NX
    xr = (g, z * NX + (x + 1) % NX)
    xl = (g, z * NX + (x + NX - 1) % NX)
    xo = (g, z * NX + (x + 2) % NX)
    sense = 1 + (NZ - 2) * (g % 2)
    zu = (g, ((z + sense) % NZ) * NX + x)
    zd = (g, ((z + NZ - sense) % NZ) * NX + x)

    halos = (
        (d < nd - 1, (g, (d + 1) % nd), d > 0),
        (d > 0, (g, (d + nd - 1) % nd), d < nd - 1),
        (g < ng - 1, ((g + 1) % ng, d), g > 0),
        (g > 0, ((g + ng - 1) % ng, d), g < ng - 1),
    )

    load_p = pltpu.make_async_copy(p_hbm, pv.at[0], in_sem.at[0])
    load_a = pltpu.make_async_copy(a_hbm, av, in_sem.at[1])
    load_p.start()
    load_a.start()

    barrier = pltpu.get_barrier_semaphore()
    expected = 5
    for peer in (xr, xl, xo, zu, zd):
        pl.semaphore_signal(barrier, inc=1, device_id=peer, device_id_type=MESH)
    for sends, peer, gets in halos:
        @pl.when(sends)
        def _():
            pl.semaphore_signal(barrier, inc=1, device_id=peer, device_id_type=MESH)

        expected = expected + jnp.where(gets, 1, 0)
    pl.semaphore_wait(barrier, expected)

    def halo_copy(i):
        return pltpu.make_async_remote_copy(
            src_ref=p_hbm,
            dst_ref=pv.at[1 + i],
            send_sem=halo_send.at[i],
            recv_sem=halo_recv.at[i],
            device_id=halos[i][1],
            device_id_type=MESH,
        )

    for i in range(4):
        @pl.when(halos[i][0])
        def _():
            halo_copy(i).start()

    def label_copy(i):
        return pltpu.make_async_remote_copy(
            src_ref=lv.at[0],
            dst_ref=lv.at[1 + i],
            send_sem=lab_send.at[i],
            recv_sem=lab_recv.at[i],
            device_id=(xr, xl, xo)[i],
            device_id_type=MESH,
        )

    def place(o, carry):
        one, two = -1, -1
        for i in range(elems):
            e = elems - 1 - i
            here = owner[0, e] == o
            two = jnp.where(here, one, two)
            one = jnp.where(here, e, one)
        first, second = jnp.maximum(one, 0), jnp.maximum(two, 0)
        name = jnp.where(one < 0, -1, agg_local[0, first])
        other = jnp.where(two < 0, -1, agg_local[0, second])
        same = jnp.logical_and(two >= 0, name == other)
        elem[2 * o] = first
        elem[2 * o + 1] = second
        twin[o] = jnp.where(same, 1, 0)
        label[0, 2 * o] = name
        label[0, 2 * o + 1] = jnp.where(same, -1, other)
        return carry

    lax.fori_loop(0, SLOTS // 2, place, 0)
    share = pltpu.make_async_copy(label, lv.at[0], lab_sem.at[1])
    share.start()
    share.wait()
    for i in range(3):
        label_copy(i).start()

    for i in range(4):
        @pl.when(jnp.logical_not(halos[i][2]))
        def _():
            def clear(e, carry):
                pv[1 + i, e] = jnp.zeros((blk, blk), BF)
                return carry

            lax.fori_loop(0, elems, clear, 0)

    for i in range(3):
        label_copy(i).wait_recv()
    load_names = pltpu.make_async_copy(lv, names, lab_sem.at[0])
    load_names.start()
    load_p.wait()
    load_a.wait()
    for i in (2, 3, 0, 1):
        @pl.when(halos[i][2])
        def _():
            halo_copy(i).wait_recv()

    def base(t, dx):
        return 2 * (((z + sense * RELS[t]) % NZ) * NX + (x + dx) % NX)

    def compute(t, dx, rows=(1, 0)):
        for k in rows:
            e = elem[base(t, dx) + k]
            own = pv[0, e]
            weighted = []
            for f in range(KC):
                face = own if f == 0 else pv[SOURCE[f], near[f - 1, e]]
                applied = jnp.dot(av[e, f], face, preferred_element_type=F32).astype(BF)
                weighted.append(
                    lax.dot_general(
                        own, applied, (((0,), (0,)), ((), ())), preferred_element_type=F32
                    )
                )
            for s in range(KC):
                total = None
                for f in range(KC):
                    term = jnp.where(slot[f, e] == s, weighted[f], 0.0)
                    total = term if total is None else total + term
                row = (t % RING) * 8 + 2 * dx
                if k == 0:
                    second = sv[row + 1, s].astype(F32)
                    total = total + jnp.where(twin[base(t, dx) // 2] == 1, second, 0.0)
                sv[row + k, s] = total.astype(BF)

    def compute_all(t):
        def one(dx, carry):
            compute(t, dx)
            return carry

        lax.fori_loop(0, NX, one, 0)

    def slots_of(p):
        return pl.ds(*SPLIT[p])

    def remote(kind, t, p, src, dst, peer):
        n = t * PIECES + p
        return pltpu.make_async_remote_copy(
            src_ref=src,
            dst_ref=dst,
            send_sem=x_send.at[kind, n],
            recv_sem=x_recv.at[kind, n],
            device_id=peer,
            device_id_type=MESH,
        )

    def first_hop(t, p):
        r = slots_of(p)
        two = pl.ds(2 * t, 2)
        q = (t % RING) * 8
        return (
            remote(0, t, p, sv.at[q + 4, r], relay.at[2 * t, r], xr),
            remote(1, t, p, sv.at[q + 5, r], relay.at[2 * t + 1, r], xl),
            remote(2, t, p, sv.at[pl.ds(q + 2, 2), r], left.at[two, r], xr),
            remote(3, t, p, sv.at[pl.ds(q + 6, 2), r], right.at[two, r], xl),
        )

    def second_hop(t, p):
        r = slots_of(p)
        return (
            remote(4, t, p, relay.at[2 * t, r], opp.at[2 * t, r], xr),
            remote(5, t, p, relay.at[2 * t + 1, r], opp.at[2 * t + 1, r], xl),
        )

    def z_copy(way, k, p):
        n = (way * 4 + k - 1) * PIECES + p
        count = 4 if k == 4 else AGG
        return pltpu.make_async_remote_copy(
            src_ref=zs.at[way, pl.ds(ZOUT[k], count), slots_of(p)],
            dst_ref=zr.at[way, pl.ds(ZIN[k], count), slots_of(p)],
            send_sem=z_send.at[n],
            recv_sem=z_recv.at[n],
            device_id=zu if way == 0 else zd,
            device_id_type=MESH,
        )

    def combine(t, p, first, count, arrived, put):
        low, slots = SPLIT[p]
        own_of = [names[src, 0, base(t, 0) + k] for src in range(4) for k in range(2)]
        rows = [(sv, (t % RING) * 8), (left, 2 * t), (right, 2 * t), (opp, 2 * t)]

        def one(i, carry):
            a = first + i
            picks = [name == a for name in own_of]

            def block(n, inner):
                s = low + n
                total = None
                for ref in arrived:
                    term = ref(i, s).astype(F32)
                    total = term if total is None else total + term
                nothing = jnp.zeros((blk, blk), BF)
                for m, (ref, q) in enumerate(rows):
                    term = lax.select(picks[2 * m + 1], ref[q + 1, s], nothing)
                    term = lax.select(picks[2 * m], ref[q, s], term).astype(F32)
                    total = term if total is None else total + term
                put(i, s, total.astype(BF))
                return inner

            return lax.fori_loop(0, slots, block, carry)

        lax.fori_loop(0, count, one, 0)

    def from_z(way, row, p):
        return lambda i, s: zr[way, row + i, s]

    def to_z(way, row, p):
        def put(i, s, value):
            zs[way, row + i, s] = value

        return put

    def step(t, p):
        rel = RELS[t]
        if rel == 4:
            for way in range(2):
                combine(t, p, 4 * way, 4, (), to_z(way, ZOUT[4], p))
                z_copy(way, 4, p).start()
        elif rel == 0:
            for way in range(2):
                z_copy(way, 1, p).wait_recv()

            def put(i, s, value):
                out[i, s] = value

            combine(t, p, 0, AGG, (from_z(0, ZIN[1], p), from_z(1, ZIN[1], p)), put)
        else:
            way, k = (0, rel) if rel < 4 else (1, NZ - rel)
            if k == 1:
                z_copy(way, 3, p).wait_send()
            z_copy(way, k + 1, p).wait_recv()
            if k == 3:
                for half in range(2):
                    arrived = (from_z(way, ZIN[4], p),) if half == way else ()
                    combine(t, p, 4 * half, 4, arrived, to_z(way, ZOUT[3] + 4 * half, p))
            else:
                combine(t, p, 0, AGG, (from_z(way, ZIN[k + 1], p),), to_z(way, ZOUT[k], p))
            z_copy(way, k, p).start()

    start_t, start_p = ORDER[0]
    hop = first_hop(start_t, start_p)
    compute(start_t, 2, (1,))
    hop[1].start()
    compute(start_t, 2, (0,))
    hop[0].start()
    compute(start_t, 1)
    hop[2].start()
    compute(start_t, 3)
    hop[3].start()
    compute(start_t, 0)
    load_names.wait()
    done = {start_t}
    for n, (t, p) in enumerate(ORDER):
        hop = first_hop(t, p)
        again = second_hop(t, p)
        for way in range(2):
            hop[way].wait_recv()
            again[way].start()
        if n + 1 < len(ORDER):
            for copy in first_hop(*ORDER[n + 1]):
                copy.start()
        if n + 2 < len(ORDER) and ORDER[n + 2][0] not in done:
            later = ORDER[n + 2][0]
            done.add(later)
            if later >= RING:
                for q in range(PIECES):
                    for copy in first_hop(later - RING, q):
                        copy.wait_send()
            compute_all(later)
        hop[2].wait_recv()
        hop[3].wait_recv()
        again[0].wait_recv()
        again[1].wait_recv()
        step(t, p)
    for t, p in ORDER:
        copies = second_hop(t, p)
        if t + RING >= NZ:
            copies = copies + first_hop(t, p)
        for copy in copies:
            copy.wait_send()
    for way in range(2):
        for k in (1, 2, 4):
            for p in range(PIECES):
                z_copy(way, k, p).wait_send()
    for i in range(3):
        label_copy(i).wait_send()
    for i in range(4):
        @pl.when(halos[i][0])
        def _():
            halo_copy(i).wait_send()


def make_coarse(owner, agg_local, near, slot, a_blocks, p_blocks):
    elems, blk, _ = p_blocks.shape
    block = (KC, blk, blk)
    n = NZ * PIECES
    smem = pl.BlockSpec(memory_space=pltpu.SMEM)
    hbm = pl.BlockSpec(memory_space=pl.ANY)
    dma = pltpu.SemaphoreType.DMA
    return pl.pallas_call(
        coarse_kernel,
        in_specs=[smem, smem, smem, smem, hbm, hbm],
        out_specs=pl.BlockSpec(memory_space=pltpu.VMEM),
        out_shape=pltpu.VMEM((AGG,) + block, BF),
        scratch_shapes=[
            pltpu.VMEM((elems,) + block, BF),
            pltpu.VMEM((5, elems, blk, blk), BF),
            pltpu.VMEM((8 * RING,) + block, BF),
            pltpu.VMEM((2 * NZ,) + block, BF),
            pltpu.VMEM((2 * NZ,) + block, BF),
            pltpu.VMEM((2 * NZ,) + block, BF),
            pltpu.VMEM((2 * NZ,) + block, BF),
            pltpu.VMEM((2, ZOUT_ROWS) + block, BF),
            pltpu.VMEM((2, ZIN_ROWS) + block, BF),
            pltpu.VMEM((4, 8, 128), I32),
            pltpu.SMEM((4, 8, 128), I32),
            pltpu.SMEM((SLOTS,), I32),
            pltpu.SMEM((SLOTS // 2,), I32),
            pltpu.SMEM((8, 128), I32),
            dma((2,)),
            dma((4,)),
            dma((4,)),
            dma((3,)),
            dma((3,)),
            dma((2,)),
            dma((6, n)),
            dma((6, n)),
            dma((n,)),
            dma((n,)),
        ],
        compiler_params=pltpu.CompilerParams(
            collective_id=0, has_side_effects=True, vmem_limit_bytes=60 << 20
        ),
        name="coarse",
    )(owner, agg_local, near, slot, a_blocks, p_blocks)


def on_device(a_blocks, p_blocks, neighbours, coarse_slot, owner, agg_local):
    return make_coarse(
        owner.T, agg_local[None, :], neighbours.T, coarse_slot.T, a_blocks, p_blocks
    )


def solution(mesh):
    placed = (
        P(("grp", "dev"), None, None, None),
        P(("grp", "dev"), None, None),
        P(("grp", "dev"), None),
        P(("grp", "dev"), None),
        P(("grp", "dev"), None),
        P(("grp", "dev")),
    )
    return jax.shard_map(
        on_device,
        mesh=mesh,
        in_specs=placed,
        out_specs=P(("grp", "dev"), None, None, None),
        check_vma=False,
    )
```

```python
import jax
import jax.numpy as jnp
from jax import lax
from jax.experimental import pallas as pl
from jax.experimental.pallas import tpu as pltpu
from jax.sharding import PartitionSpec as P

KC = 7
NX = 4
NZ = 8
AGG = 8
SLOTS = 2 * NX * NZ
SPLIT = ((0, 4), (4, 3))
PIECES = len(SPLIT)
RING = 4
AHEAD = 2
MESH = pl.DeviceIdType.MESH
BF = jnp.bfloat16
F32 = jnp.float32
I32 = jnp.int32

RELS = (4, 3, 5, 2, 6, 1, 7, 0)
ORDER = tuple(
    (t, p)
    for group in ((0,), (1, 2), (3, 4), (5, 6), (7,))
    for p in range(PIECES)
    for t in group
)
ZIN = {4: 0, 3: 4, 2: 12, 1: 20}
ZIN_ROWS = 28
ZOUT = {4: 0, 3: 4, 2: 12, 1: 4}
ZOUT_ROWS = 20
SOURCE = (0, 0, 0, 1, 2, 3, 4)


def coarse_kernel(
    owner_hbm, agg_hbm, near_hbm, slot_hbm, a_hbm, p_hbm, out,
    av, pv, sv, left, right, opp, zs, zr, lv, names, elem, twin, label,
    owner, agg_local, near, slot,
    in_sem, index_sem, halo_send, halo_recv, lab_send, lab_recv, lab_sem, x_send, x_recv, z_send, z_recv,
):
    elems, blk, _ = p_hbm.shape
    ng, nd = lax.axis_size("grp"), lax.axis_size("dev")
    g = lax.axis_index("grp")
    d = lax.axis_index("dev")
    z = d // NX
    x = d % NX
    xr = (g, z * NX + (x + 1) % NX)
    xl = (g, z * NX + (x + NX - 1) % NX)
    xo = (g, z * NX + (x + 2) % NX)
    sense = 1 + (NZ - 2) * (g % 2)
    zu = (g, ((z + sense) % NZ) * NX + x)
    zd = (g, ((z + NZ - sense) % NZ) * NX + x)

    halos = (
        (d < nd - 1, (g, (d + 1) % nd), d > 0),
        (d > 0, (g, (d + nd - 1) % nd), d < nd - 1),
        (g < ng - 1, ((g + 1) % ng, d), g > 0),
        (g > 0, ((g + ng - 1) % ng, d), g < ng - 1),
    )

    load_p = pltpu.make_async_copy(p_hbm, pv.at[0], in_sem.at[0])
    load_a = pltpu.make_async_copy(a_hbm, av, in_sem.at[1])
    indices = tuple(
        pltpu.make_async_copy(source, target, index_sem.at[i])
        for i, (source, target) in enumerate(
            ((owner_hbm, owner), (agg_hbm, agg_local), (near_hbm, near), (slot_hbm, slot))
        )
    )
    for copy in indices:
        copy.start()
    load_p.start()
    load_a.start()

    barrier = pltpu.get_barrier_semaphore()
    expected = 5
    for peer in (xr, xl, xo, zu, zd):
        pl.semaphore_signal(barrier, inc=1, device_id=peer, device_id_type=MESH)
    for has_receiver, peer, gets in halos:
        @pl.when(has_receiver)
        def _():
            pl.semaphore_signal(barrier, inc=1, device_id=peer, device_id_type=MESH)

        expected = expected + jnp.where(gets, 1, 0)
    pl.semaphore_wait(barrier, expected)

    def halo_copy(i):
        return pltpu.make_async_remote_copy(
            src_ref=p_hbm,
            dst_ref=pv.at[1 + i],
            send_sem=halo_send.at[i],
            recv_sem=halo_recv.at[i],
            device_id=halos[i][1],
            device_id_type=MESH,
        )

    for i in range(4):
        @pl.when(halos[i][0])
        def _():
            halo_copy(i).start()

    def label_copy(i):
        return pltpu.make_async_remote_copy(
            src_ref=lv.at[0],
            dst_ref=lv.at[1 + i],
            send_sem=lab_send.at[i],
            recv_sem=lab_recv.at[i],
            device_id=(xr, xl, xo)[i],
            device_id_type=MESH,
        )

    def place(o, carry):
        one, two = -1, -1
        for i in range(elems):
            e = elems - 1 - i
            here = owner[0, e] == o
            two = jnp.where(here, one, two)
            one = jnp.where(here, e, one)
        first, second = jnp.maximum(one, 0), jnp.maximum(two, 0)
        name = jnp.where(one < 0, -1, agg_local[0, first])
        other = jnp.where(two < 0, -1, agg_local[0, second])
        same = jnp.logical_and(two >= 0, name == other)
        elem[2 * o] = first
        elem[2 * o + 1] = second
        twin[o] = jnp.where(same, 1, 0)
        label[0, 2 * o] = name
        label[0, 2 * o + 1] = jnp.where(same, -1, other)
        return carry

    for copy in indices:
        copy.wait()
    lax.fori_loop(0, SLOTS // 2, place, 0)
    share = pltpu.make_async_copy(label, lv.at[0], lab_sem.at[1])
    share.start()
    share.wait()
    for i in range(3):
        label_copy(i).start()

    for i in range(4):
        @pl.when(jnp.logical_not(halos[i][2]))
        def _():
            def clear(e, carry):
                pv[1 + i, e] = jnp.zeros((blk, blk), BF)
                return carry

            lax.fori_loop(0, elems, clear, 0)

    for i in range(3):
        label_copy(i).wait_recv()
    load_names = pltpu.make_async_copy(lv, names, lab_sem.at[0])
    load_names.start()
    load_p.wait()
    load_a.wait()
    for i in (2, 3, 0, 1):
        @pl.when(halos[i][2])
        def _():
            halo_copy(i).wait_recv()

    def base(t, dx):
        return 2 * (((z + sense * RELS[t]) % NZ) * NX + (x + dx) % NX)

    def compute(t, dx):
        for k in (1, 0):
            e = elem[base(t, dx) + k]
            own = pv[0, e]
            weighted = []
            for f in range(KC):
                face = own if f == 0 else pv[SOURCE[f], near[f - 1, e]]
                applied = jnp.dot(av[e, f], face, preferred_element_type=F32).astype(BF)
                weighted.append(
                    lax.dot_general(
                        own, applied, (((0,), (0,)), ((), ())), preferred_element_type=F32
                    )
                )
            for s in range(KC):
                total = None
                for f in range(KC):
                    term = jnp.where(slot[f, e] == s, weighted[f], 0.0)
                    total = term if total is None else total + term
                row = (t % RING) * 8 + 2 * dx
                if k == 0:
                    second = sv[row + 1, s].astype(F32)
                    total = total + jnp.where(twin[base(t, dx) // 2] == 1, second, 0.0)
                sv[row + k, s] = total.astype(BF)

    def compute_all(t):
        def one(dx, carry):
            compute(t, dx)
            return carry

        lax.fori_loop(0, NX, one, 0)

    def slots_of(p):
        return pl.ds(*SPLIT[p])

    def remote(kind, t, p, src, dst, peer):
        n = t * PIECES + p
        return pltpu.make_async_remote_copy(
            src_ref=src,
            dst_ref=dst,
            send_sem=x_send.at[kind, n],
            recv_sem=x_recv.at[kind, n],
            device_id=peer,
            device_id_type=MESH,
        )

    def sends(t, p):
        r = slots_of(p)
        two = pl.ds(2 * t, 2)
        q = (t % RING) * 8
        return (
            remote(0, t, p, sv.at[pl.ds(q + 4, 2), r], opp.at[two, r], xo),
            remote(1, t, p, sv.at[pl.ds(q + 2, 2), r], left.at[two, r], xr),
            remote(2, t, p, sv.at[pl.ds(q + 6, 2), r], right.at[two, r], xl),
        )

    def z_copy(way, k, p):
        n = (way * 4 + k - 1) * PIECES + p
        count = 4 if k == 4 else AGG
        return pltpu.make_async_remote_copy(
            src_ref=zs.at[way, pl.ds(ZOUT[k], count), slots_of(p)],
            dst_ref=zr.at[way, pl.ds(ZIN[k], count), slots_of(p)],
            send_sem=z_send.at[n],
            recv_sem=z_recv.at[n],
            device_id=zu if way == 0 else zd,
            device_id_type=MESH,
        )

    def combine(t, p, first, count, arrived, put):
        low, slots = SPLIT[p]
        own_of = [names[src, 0, base(t, 0) + k] for src in range(4) for k in range(2)]
        rows = [(sv, (t % RING) * 8), (left, 2 * t), (right, 2 * t), (opp, 2 * t)]

        def one(i, carry):
            a = first + i
            picks = [name == a for name in own_of]

            def block(n, inner):
                s = low + n
                total = None
                for ref in arrived:
                    term = ref(i, s).astype(F32)
                    total = term if total is None else total + term
                nothing = jnp.zeros((blk, blk), BF)
                for m, (ref, q) in enumerate(rows):
                    term = lax.select(picks[2 * m + 1], ref[q + 1, s], nothing)
                    term = lax.select(picks[2 * m], ref[q, s], term).astype(F32)
                    total = term if total is None else total + term
                put(i, s, total.astype(BF))
                return inner

            return lax.fori_loop(0, slots, block, carry)

        lax.fori_loop(0, count, one, 0)

    def from_z(way, row, p):
        return lambda i, s: zr[way, row + i, s]

    def to_z(way, row, p):
        def put(i, s, value):
            zs[way, row + i, s] = value

        return put

    def step(t, p):
        rel = RELS[t]
        if rel == 4:
            for way in range(2):
                combine(t, p, 4 * way, 4, (), to_z(way, ZOUT[4], p))
                z_copy(way, 4, p).start()
        elif rel == 0:
            for way in range(2):
                z_copy(way, 1, p).wait_recv()

            def put(i, s, value):
                out[i, s] = value

            combine(t, p, 0, AGG, (from_z(0, ZIN[1], p), from_z(1, ZIN[1], p)), put)
        else:
            way, k = (0, rel) if rel < 4 else (1, NZ - rel)
            if k == 1:
                z_copy(way, 3, p).wait_send()
            z_copy(way, k + 1, p).wait_recv()
            if k == 3:
                for half in range(2):
                    arrived = (from_z(way, ZIN[4], p),) if half == way else ()
                    combine(t, p, 4 * half, 4, arrived, to_z(way, ZOUT[3] + 4 * half, p))
            else:
                combine(t, p, 0, AGG, (from_z(way, ZIN[k + 1], p),), to_z(way, ZOUT[k], p))
            z_copy(way, k, p).start()

    def issue(n):
        for copy in sends(*ORDER[n]):
            copy.start()

    done = set()

    def prepare(n):
        if n >= len(ORDER) or ORDER[n][0] in done:
            return
        t = ORDER[n][0]
        done.add(t)
        if t >= RING:
            for p in range(PIECES):
                for copy in sends(t - RING, p):
                    copy.wait_send()
        compute_all(t)

    start_t = ORDER[0][0]
    done.add(start_t)
    for dx, copy in zip((2, 1, 3), sends(*ORDER[0])):
        compute(start_t, dx)
        copy.start()
    compute(start_t, 0)
    for n in range(1, AHEAD):
        prepare(n)
        issue(n)
    prepare(AHEAD)
    load_names.wait()
    for n, (t, p) in enumerate(ORDER):
        if n + AHEAD < len(ORDER):
            issue(n + AHEAD)
        prepare(n + AHEAD + 1)
        for copy in sends(t, p):
            copy.wait_recv()
        step(t, p)
    for t, p in ORDER:
        if t + RING >= NZ:
            for copy in sends(t, p):
                copy.wait_send()
    for way in range(2):
        for k in (1, 2, 4):
            for p in range(PIECES):
                z_copy(way, k, p).wait_send()
    for i in range(3):
        label_copy(i).wait_send()
    for i in range(4):
        @pl.when(halos[i][0])
        def _():
            halo_copy(i).wait_send()


def make_coarse(owner, agg_local, near, slot, a_blocks, p_blocks):
    elems, blk, _ = p_blocks.shape
    block = (KC, blk, blk)
    n = NZ * PIECES
    hbm = pl.BlockSpec(memory_space=pl.ANY)
    dma = pltpu.SemaphoreType.DMA
    return pl.pallas_call(
        coarse_kernel,
        in_specs=[hbm] * 6,
        out_specs=pl.BlockSpec(memory_space=pltpu.VMEM),
        out_shape=pltpu.VMEM((AGG,) + block, BF),
        scratch_shapes=[
            pltpu.VMEM((elems,) + block, BF),
            pltpu.VMEM((5, elems, blk, blk), BF),
            pltpu.VMEM((8 * RING,) + block, BF),
            pltpu.VMEM((2 * NZ,) + block, BF),
            pltpu.VMEM((2 * NZ,) + block, BF),
            pltpu.VMEM((2 * NZ,) + block, BF),
            pltpu.VMEM((2, ZOUT_ROWS) + block, BF),
            pltpu.VMEM((2, ZIN_ROWS) + block, BF),
            pltpu.VMEM((4, 8, 128), I32),
            pltpu.SMEM((4, 8, 128), I32),
            pltpu.SMEM((SLOTS,), I32),
            pltpu.SMEM((SLOTS // 2,), I32),
            pltpu.SMEM((8, 128), I32),
            pltpu.SMEM(owner.shape, I32),
            pltpu.SMEM(agg_local.shape, I32),
            pltpu.SMEM(near.shape, I32),
            pltpu.SMEM(slot.shape, I32),
            dma((2,)),
            dma((4,)),
            dma((4,)),
            dma((4,)),
            dma((3,)),
            dma((3,)),
            dma((2,)),
            dma((3, n)),
            dma((3, n)),
            dma((n,)),
            dma((n,)),
        ],
        compiler_params=pltpu.CompilerParams(
            collective_id=0, has_side_effects=True, vmem_limit_bytes=60 << 20
        ),
        name="coarse",
    )(owner, agg_local, near, slot, a_blocks, p_blocks)


def on_device(a_blocks, p_blocks, neighbours, coarse_slot, owner, agg_local):
    return make_coarse(
        owner.T, agg_local[None, :], neighbours.T, coarse_slot.T, a_blocks, p_blocks
    )


def solution(mesh):
    placed = (
        P(("grp", "dev"), None, None, None),
        P(("grp", "dev"), None, None),
        P(("grp", "dev"), None),
        P(("grp", "dev"), None),
        P(("grp", "dev"), None),
        P(("grp", "dev")),
    )
    return jax.shard_map(
        on_device,
        mesh=mesh,
        in_specs=placed,
        out_specs=P(("grp", "dev"), None, None, None),
        check_vma=False,
    )
```

```python
import jax
import jax.numpy as jnp
from jax import lax
from jax.experimental import pallas as pl
from jax.experimental.pallas import tpu as pltpu
from jax.sharding import PartitionSpec as P

KC = 7
NX = 4
NZ = 8
AGG = 8
SLOTS = 2 * NX * NZ
SPLIT = ((0, 4), (4, 3))
PIECES = len(SPLIT)
RING = 4
AHEAD = 2
MESH = pl.DeviceIdType.MESH
BF = jnp.bfloat16
F32 = jnp.float32
I32 = jnp.int32

RELS = (4, 3, 5, 2, 6, 1, 7, 0)
ORDER = tuple(
    (t, p)
    for group in ((0,), (1, 2), (3, 4), (5, 6), (7,))
    for p in range(PIECES)
    for t in group
)
ZIN = {4: 0, 3: 4, 2: 12, 1: 20}
ZIN_ROWS = 28
ZOUT = {4: 0, 3: 4, 2: 12, 1: 4}
ZOUT_ROWS = 20
SOURCE = (0, 0, 0, 1, 2, 3, 4)


def coarse_kernel(
    owner_hbm, agg_hbm, near_hbm, slot_hbm, a_hbm, p_hbm, out,
    av, pv, sv, left, right, opp, zs, zr, lv, names, elem, twin, label,
    owner, agg_local, near, slot,
    in_sem, index_sem, halo_send, halo_recv, lab_send, lab_recv, lab_sem, x_send, x_recv, z_send, z_recv,
):
    elems, blk, _ = p_hbm.shape
    ng, nd = lax.axis_size("grp"), lax.axis_size("dev")
    g = lax.axis_index("grp")
    d = lax.axis_index("dev")
    z = d // NX
    x = d % NX
    xr = (g, z * NX + (x + 1) % NX)
    xl = (g, z * NX + (x + NX - 1) % NX)
    xo = (g, z * NX + (x + 2) % NX)
    sense = 1 + (NZ - 2) * (g % 2)
    zu = (g, ((z + sense) % NZ) * NX + x)
    zd = (g, ((z + NZ - sense) % NZ) * NX + x)

    halos = (
        (d < nd - 1, (g, (d + 1) % nd), d > 0),
        (d > 0, (g, (d + nd - 1) % nd), d < nd - 1),
        (g < ng - 1, ((g + 1) % ng, d), g > 0),
        (g > 0, ((g + ng - 1) % ng, d), g < ng - 1),
    )

    load_p = pltpu.make_async_copy(p_hbm, pv.at[0], in_sem.at[0])
    load_a = pltpu.make_async_copy(a_hbm, av, in_sem.at[1])
    indices = tuple(
        pltpu.make_async_copy(source, target, index_sem.at[i])
        for i, (source, target) in enumerate(
            ((owner_hbm, owner), (agg_hbm, agg_local), (near_hbm, near), (slot_hbm, slot))
        )
    )
    for copy in indices:
        copy.start()
    load_p.start()
    load_a.start()

    barrier = pltpu.get_barrier_semaphore()
    expected = 5
    for peer in (xr, xl, xo, zu, zd):
        pl.semaphore_signal(barrier, inc=1, device_id=peer, device_id_type=MESH)
    for has_receiver, peer, gets in halos:
        @pl.when(has_receiver)
        def _():
            pl.semaphore_signal(barrier, inc=1, device_id=peer, device_id_type=MESH)

        expected = expected + jnp.where(gets, 1, 0)
    pl.semaphore_wait(barrier, expected)

    def halo_copy(i):
        return pltpu.make_async_remote_copy(
            src_ref=p_hbm,
            dst_ref=pv.at[1 + i],
            send_sem=halo_send.at[i],
            recv_sem=halo_recv.at[i],
            device_id=halos[i][1],
            device_id_type=MESH,
        )

    for i in range(4):
        @pl.when(halos[i][0])
        def _():
            halo_copy(i).start()

    def label_copy(i):
        return pltpu.make_async_remote_copy(
            src_ref=lv.at[0],
            dst_ref=lv.at[1 + i],
            send_sem=lab_send.at[i],
            recv_sem=lab_recv.at[i],
            device_id=(xr, xl, xo)[i],
            device_id_type=MESH,
        )

    def place(o, carry):
        one, two = -1, -1
        for i in range(elems):
            e = elems - 1 - i
            here = owner[0, e] == o
            two = jnp.where(here, one, two)
            one = jnp.where(here, e, one)
        first, second = jnp.maximum(one, 0), jnp.maximum(two, 0)
        name = jnp.where(one < 0, -1, agg_local[0, first])
        other = jnp.where(two < 0, -1, agg_local[0, second])
        same = jnp.logical_and(two >= 0, name == other)
        elem[2 * o] = first
        elem[2 * o + 1] = second
        twin[o] = jnp.where(same, 1, 0)
        label[0, 2 * o] = name
        label[0, 2 * o + 1] = jnp.where(same, -1, other)
        return carry

    for copy in indices:
        copy.wait()
    lax.fori_loop(0, SLOTS // 2, place, 0)
    share = pltpu.make_async_copy(label, lv.at[0], lab_sem.at[1])
    share.start()
    share.wait()
    for i in range(3):
        label_copy(i).start()

    for i in range(4):
        @pl.when(jnp.logical_not(halos[i][2]))
        def _():
            def clear(e, carry):
                pv[1 + i, e] = jnp.zeros((blk, blk), BF)
                return carry

            lax.fori_loop(0, elems, clear, 0)

    load_p.wait()
    load_a.wait()
    for i in (2, 3, 0, 1):
        @pl.when(halos[i][2])
        def _():
            halo_copy(i).wait_recv()

    def base(t, dx):
        return 2 * (((z + sense * RELS[t]) % NZ) * NX + (x + dx) % NX)

    def compute(t, dx):
        for k in (1, 0):
            e = elem[base(t, dx) + k]
            own = pv[0, e]
            weighted = []
            for f in range(KC):
                face = own if f == 0 else pv[SOURCE[f], near[f - 1, e]]
                applied = jnp.dot(av[e, f], face, preferred_element_type=F32).astype(BF)
                weighted.append(
                    lax.dot_general(
                        own, applied, (((0,), (0,)), ((), ())), preferred_element_type=F32
                    )
                )
            for s in range(KC):
                total = None
                for f in range(KC):
                    term = jnp.where(slot[f, e] == s, weighted[f], 0.0)
                    total = term if total is None else total + term
                row = (t % RING) * 8 + 2 * dx
                if k == 0:
                    second = sv[row + 1, s].astype(F32)
                    total = total + jnp.where(twin[base(t, dx) // 2] == 1, second, 0.0)
                sv[row + k, s] = total.astype(BF)

    def compute_all(t):
        def one(dx, carry):
            compute(t, dx)
            return carry

        lax.fori_loop(0, NX, one, 0)

    def slots_of(p):
        return pl.ds(*SPLIT[p])

    def remote(kind, t, p, src, dst, peer):
        n = t * PIECES + p
        return pltpu.make_async_remote_copy(
            src_ref=src,
            dst_ref=dst,
            send_sem=x_send.at[kind, n],
            recv_sem=x_recv.at[kind, n],
            device_id=peer,
            device_id_type=MESH,
        )

    def sends(t, p):
        r = slots_of(p)
        two = pl.ds(2 * t, 2)
        q = (t % RING) * 8
        return (
            remote(0, t, p, sv.at[pl.ds(q + 4, 2), r], opp.at[two, r], xo),
            remote(1, t, p, sv.at[pl.ds(q + 2, 2), r], left.at[two, r], xr),
            remote(2, t, p, sv.at[pl.ds(q + 6, 2), r], right.at[two, r], xl),
        )

    def z_copy(way, k, p):
        n = (way * 4 + k - 1) * PIECES + p
        count = 4 if k == 4 else AGG
        return pltpu.make_async_remote_copy(
            src_ref=zs.at[way, pl.ds(ZOUT[k], count), slots_of(p)],
            dst_ref=zr.at[way, pl.ds(ZIN[k], count), slots_of(p)],
            send_sem=z_send.at[n],
            recv_sem=z_recv.at[n],
            device_id=zu if way == 0 else zd,
            device_id_type=MESH,
        )

    def combine(t, p, first, count, arrived, put):
        low, slots = SPLIT[p]
        own_of = [names[src, 0, base(t, 0) + k] for src in range(4) for k in range(2)]
        rows = [(sv, (t % RING) * 8), (left, 2 * t), (right, 2 * t), (opp, 2 * t)]

        def one(i, carry):
            a = first + i
            picks = [name == a for name in own_of]

            def block(n, inner):
                s = low + n
                total = None
                for ref in arrived:
                    term = ref(i, s).astype(F32)
                    total = term if total is None else total + term
                nothing = jnp.zeros((blk, blk), BF)
                for m, (ref, q) in enumerate(rows):
                    term = lax.select(picks[2 * m + 1], ref[q + 1, s], nothing)
                    term = lax.select(picks[2 * m], ref[q, s], term).astype(F32)
                    total = term if total is None else total + term
                put(i, s, total.astype(BF))
                return inner

            return lax.fori_loop(0, slots, block, carry)

        lax.fori_loop(0, count, one, 0)

    def from_z(way, row, p):
        return lambda i, s: zr[way, row + i, s]

    def to_z(way, row, p):
        def put(i, s, value):
            zs[way, row + i, s] = value

        return put

    def step(t, p):
        rel = RELS[t]
        if rel == 4:
            for way in range(2):
                combine(t, p, 4 * way, 4, (), to_z(way, ZOUT[4], p))
                z_copy(way, 4, p).start()
        elif rel == 0:
            for way in range(2):
                z_copy(way, 1, p).wait_recv()

            def put(i, s, value):
                out[i, s] = value

            combine(t, p, 0, AGG, (from_z(0, ZIN[1], p), from_z(1, ZIN[1], p)), put)
        else:
            way, k = (0, rel) if rel < 4 else (1, NZ - rel)
            if k == 1:
                z_copy(way, 3, p).wait_send()
            z_copy(way, k + 1, p).wait_recv()
            if k == 3:
                for half in range(2):
                    arrived = (from_z(way, ZIN[4], p),) if half == way else ()
                    combine(t, p, 4 * half, 4, arrived, to_z(way, ZOUT[3] + 4 * half, p))
            else:
                combine(t, p, 0, AGG, (from_z(way, ZIN[k + 1], p),), to_z(way, ZOUT[k], p))
            z_copy(way, k, p).start()

    def issue(n):
        for copy in sends(*ORDER[n]):
            copy.start()

    done = set()

    def prepare(n):
        if n >= len(ORDER) or ORDER[n][0] in done:
            return
        t = ORDER[n][0]
        done.add(t)
        if t >= RING:
            for p in range(PIECES):
                for copy in sends(t - RING, p):
                    copy.wait_send()
        compute_all(t)

    start_t = ORDER[0][0]
    done.add(start_t)
    for dx, copy in zip((2, 1, 3), sends(*ORDER[0])):
        compute(start_t, dx)
        copy.start()
    compute(start_t, 0)
    for n in range(1, AHEAD):
        prepare(n)
        issue(n)
    prepare(AHEAD)
    for i in range(3):
        label_copy(i).wait_recv()
    load_names = pltpu.make_async_copy(lv, names, lab_sem.at[0])
    load_names.start()
    load_names.wait()
    for n, (t, p) in enumerate(ORDER):
        if n + AHEAD < len(ORDER):
            issue(n + AHEAD)
        prepare(n + AHEAD + 1)
        for copy in sends(t, p):
            copy.wait_recv()
        step(t, p)
    for t, p in ORDER:
        if t + RING >= NZ:
            for copy in sends(t, p):
                copy.wait_send()
    for way in range(2):
        for k in (1, 2, 4):
            for p in range(PIECES):
                z_copy(way, k, p).wait_send()
    for i in range(3):
        label_copy(i).wait_send()
    for i in range(4):
        @pl.when(halos[i][0])
        def _():
            halo_copy(i).wait_send()


def make_coarse(owner, agg_local, near, slot, a_blocks, p_blocks):
    elems, blk, _ = p_blocks.shape
    block = (KC, blk, blk)
    n = NZ * PIECES
    hbm = pl.BlockSpec(memory_space=pl.ANY)
    dma = pltpu.SemaphoreType.DMA
    return pl.pallas_call(
        coarse_kernel,
        in_specs=[hbm] * 6,
        out_specs=pl.BlockSpec(memory_space=pltpu.VMEM),
        out_shape=pltpu.VMEM((AGG,) + block, BF),
        scratch_shapes=[
            pltpu.VMEM((elems,) + block, BF),
            pltpu.VMEM((5, elems, blk, blk), BF),
            pltpu.VMEM((8 * RING,) + block, BF),
            pltpu.VMEM((2 * NZ,) + block, BF),
            pltpu.VMEM((2 * NZ,) + block, BF),
            pltpu.VMEM((2 * NZ,) + block, BF),
            pltpu.VMEM((2, ZOUT_ROWS) + block, BF),
            pltpu.VMEM((2, ZIN_ROWS) + block, BF),
            pltpu.VMEM((4, 8, 128), I32),
            pltpu.SMEM((4, 8, 128), I32),
            pltpu.SMEM((SLOTS,), I32),
            pltpu.SMEM((SLOTS // 2,), I32),
            pltpu.SMEM((8, 128), I32),
            pltpu.SMEM(owner.shape, I32),
            pltpu.SMEM(agg_local.shape, I32),
            pltpu.SMEM(near.shape, I32),
            pltpu.SMEM(slot.shape, I32),
            dma((2,)),
            dma((4,)),
            dma((4,)),
            dma((4,)),
            dma((3,)),
            dma((3,)),
            dma((2,)),
            dma((3, n)),
            dma((3, n)),
            dma((n,)),
            dma((n,)),
        ],
        compiler_params=pltpu.CompilerParams(
            collective_id=0, has_side_effects=True, vmem_limit_bytes=60 << 20
        ),
        name="coarse",
    )(owner, agg_local, near, slot, a_blocks, p_blocks)


def on_device(a_blocks, p_blocks, neighbours, coarse_slot, owner, agg_local):
    return make_coarse(
        owner.T, agg_local[None, :], neighbours.T, coarse_slot.T, a_blocks, p_blocks
    )


def solution(mesh):
    placed = (
        P(("grp", "dev"), None, None, None),
        P(("grp", "dev"), None, None),
        P(("grp", "dev"), None),
        P(("grp", "dev"), None),
        P(("grp", "dev"), None),
        P(("grp", "dev")),
    )
    return jax.shard_map(
        on_device,
        mesh=mesh,
        in_specs=placed,
        out_specs=P(("grp", "dev"), None, None, None),
        check_vma=False,
    )
```
